32 devices in a mesh: tm: 4 (over x, core), anta: 4 (over z), antb: 2 (over y).
Axes of the slice: x: 2, y: 2, z: 4, core: 2. Of those that a mesh axis runs over, the one named last changes fastest.
Arguments:
- samples: bfloat16 [2, 512, 6144], P('antb', 'anta', 'tm'), may hold values from -6 to 6
Outputs:
- correlation: float32 [256, 2, 512, 2, 512], P('tm', None, 'anta', 'antb')
The draws below stay inside these ranges and needn't reach their ends.
All inputs are finite; a program needn't handle non-finite values.
Results may differ from the reference program's by a relative error of at most 0.0003.
Values may be sent and summed in bfloat16 or wider, within the bound.
No kernel may reach another device: no remote copies, remote signals or barrier semaphores. Data moves between devices by JAX's collectives and lax.ppermute only.
A program may use at most 128 MiB of HBM per device.

```python
import math
import jax
import jax.numpy as jnp
from jax import lax

ANTENNA_COUNT = 512
POLARISATION_NUM = 2
LAG_TOTAL = 256
TIME = 6144


def block_levels(rng, extent, pieces, smallest, largest):
    gain, own = 1.0, jax.random.fold_in(rng, 6)
    for position, blocks in pieces:
        steps = jnp.exp(jax.random.uniform(jax.random.fold_in(own, position), (blocks,), jnp.float32, smallest / len(pieces), largest / len(pieces)))
        gain = gain * jnp.repeat(steps, extent[position] // blocks).reshape([-1 if axis == position else 1 for axis in range(len(extent))])
    return gain


def centred(own_key, shape, spread, most, cuts=(), kind=jnp.bfloat16):
    array = spread * jax.random.normal(own_key, shape, jnp.float32)
    if cuts:
        array = array * block_levels(own_key, shape, cuts, -0.22, 0.18)
    return jnp.clip(array, -most, most).astype(kind)


def setup_inputs(seed: int = 0) -> dict:
    key_of = jax.random.split(jax.random.key(seed), 2)
    samples = centred(key_of[0], (POLARISATION_NUM, ANTENNA_COUNT, TIME), 1.0, 6.0, ((0, 2), (1, 4), (2, 4)))
    return dict(samples=samples)


def reference(samples):
    flat_samples = samples.reshape(POLARISATION_NUM * ANTENNA_COUNT, TIME)
    padded = jnp.pad(flat_samples, ((0, 0), (0, LAG_TOTAL)))

    def one_lag(lag_index):
        shifted = lax.dynamic_slice_in_dim(padded, lag_index, TIME, 1)
        return jnp.dot(flat_samples, shifted.T, preferred_element_type=jnp.float32)
    lagged = lax.map(one_lag, jnp.arange(LAG_TOTAL, dtype=jnp.int32))
    return (lagged * (1.0 / math.sqrt(TIME))).reshape(LAG_TOTAL, POLARISATION_NUM, ANTENNA_COUNT, POLARISATION_NUM, ANTENNA_COUNT)
```

```python
import math

import jax
import jax.numpy as jnp
from jax import lax
from jax.experimental import pallas as pl
from jax.experimental.pallas import tpu as pltpu
from jax.sharding import PartitionSpec as P

POLARISATION_NUM = 2
LAG_TOTAL = 256
FINE = 16
PER_STEP = 2
LANES = 128
STRIP = 16


def lag_kernel(row_ref, col_ref, *refs, coarse, factor, lag_portion, parts, part_of):
    *prev, out_ref, state_ref, shifted_ref, wide_ref = refs
    row_count, window = row_ref.shape
    col_count = col_ref.shape[1]
    part_chunks = col_count // LANES
    chunks = part_chunks * parts
    lag_start = lax.axis_index("tm") * lag_portion
    first_chunk = part_of() * part_chunks

    @pl.when(pl.program_id(0) == 0)
    def _():
        state_ref[:, window:] = jnp.zeros((row_count, LANES), jnp.bfloat16)
        wide_ref[window:, :] = jnp.zeros((LAG_TOTAL, col_count), jnp.bfloat16)

        def fill_rows(index, carry):
            at = pl.multiple_of(index * STRIP, STRIP)
            state_ref[pl.ds(at, STRIP), :window] = row_ref[pl.ds(at, STRIP), :]
            return carry

        def fill_cols(index, carry):
            at = pl.multiple_of(index * LANES, LANES)
            wide_ref[pl.ds(at, LANES), :] = col_ref[pl.ds(at, LANES), :]
            return carry

        lax.fori_loop(0, row_count // STRIP, fill_rows, 0)
        lax.fori_loop(0, window // LANES, fill_cols, 0)

    def shift_strip(index, carry):
        at = pl.multiple_of(index * STRIP, STRIP)
        wide = state_ref[pl.ds(at, STRIP), :].astype(jnp.float32)
        for step in range(PER_STEP):
            to = pl.multiple_of(step * row_count + index * STRIP, STRIP)
            shifted_ref[pl.ds(to, STRIP), :] = wide[:, :window].astype(jnp.bfloat16)
            wide = pltpu.roll(wide, 1, 1)
        state_ref[pl.ds(at, STRIP), :] = wide.astype(jnp.bfloat16)
        return carry

    lax.fori_loop(0, row_count // STRIP, shift_strip, 0)

    def coarse_lag(step, carry):
        start = pl.multiple_of(lag_start + step * FINE, FINE)
        product = jnp.dot(
            shifted_ref[...], wide_ref[pl.ds(start, window), :], preferred_element_type=jnp.float32
        ) * factor
        for fine in range(PER_STEP):
            if prev:
                out_ref[step, fine] = prev[0][step, fine]
            for chunk in range(part_chunks):
                out_ref[step, fine, pl.ds(first_chunk + chunk, row_count, stride=chunks), :] = product[
                    fine * row_count : (fine + 1) * row_count, chunk * LANES : (chunk + 1) * LANES
                ]
        return carry

    lax.fori_loop(0, coarse, coarse_lag, 0)


def lag_products(rows, columns, prev, lag_portion, parts, part_of):
    row_count, window = rows.shape
    col_count = columns.shape[1]
    coarse = lag_portion // FINE
    out_rows = row_count * parts * (col_count // LANES)

    def kernel(*refs):
        lag_kernel(
            *refs, coarse=coarse, factor=1.0 / math.sqrt(window), lag_portion=lag_portion,
            parts=parts, part_of=part_of,
        )

    whole = pl.BlockSpec(memory_space=pltpu.VMEM)
    block = pl.BlockSpec((coarse, PER_STEP, out_rows, LANES), lambda m: (0, m, 0, 0))
    return pl.pallas_call(
        kernel,
        grid=(FINE // PER_STEP,),
        in_specs=[whole, whole] + [block] * len(prev),
        out_specs=block,
        out_shape=jax.ShapeDtypeStruct((coarse, FINE, out_rows, LANES), jnp.float32),
        scratch_shapes=[
            pltpu.VMEM((row_count, window + LANES), jnp.bfloat16),
            pltpu.VMEM((PER_STEP * row_count, window), jnp.bfloat16),
            pltpu.VMEM((window + LAG_TOTAL, col_count), jnp.bfloat16),
        ],
        input_output_aliases={2: 0} if prev else {},
        compiler_params=pltpu.CompilerParams(vmem_limit_bytes=56 * 1024 * 1024),
        name="lag_products",
    )(rows, columns, *prev)


def swap(array, axis, distance, size):
    return lax.ppermute(array, axis, [(i, (i + distance) % size) for i in range(size)])


def per_device(samples):
    own = samples[0]
    own_antennas, block_len = own.shape
    tm_size = lax.axis_size("tm")
    anta_size = lax.axis_size("anta")
    lag_portion = LAG_TOTAL // tm_size
    antenna_total = own_antennas * anta_size
    half = anta_size // 2
    anta_at = lax.axis_index("anta")

    other = swap(own, "antb", 1, POLARISATION_NUM)
    first = lax.axis_index("antb") == 0
    both = jnp.concatenate([jnp.where(first, own, other), jnp.where(first, other, own)], 0)
    rows = lax.all_gather(both, "tm", axis=1, tiled=True)

    turned = own.T
    if half == 2:
        pairs = [(i, i ^ 1) for i in range(anta_size)]
        beside = lax.ppermute(turned, "anta", pairs)
        even = anta_at % 2 == 0
        near = jnp.concatenate([jnp.where(even, turned, beside), jnp.where(even, beside, turned)], 1)
    else:
        groups = [list(range(half)), list(range(half, anta_size))]
        near = lax.all_gather(turned, "anta", axis=1, tiled=True, axis_index_groups=groups)
    far = swap(near, "anta", half, anta_size)
    near_columns = lax.all_gather(near, "tm", axis=0, tiled=True)
    far_columns = lax.all_gather(far, "tm", axis=0, tiled=True)

    def near_part():
        return lax.axis_index("anta") // half

    def far_part():
        return 1 - lax.axis_index("anta") // half

    out = lag_products(rows, near_columns, (), lag_portion, 2, near_part)
    out = lag_products(rows, far_columns, (out,), lag_portion, 2, far_part)
    return out.reshape(lag_portion, POLARISATION_NUM, own_antennas, 1, antenna_total)


def solution(mesh):
    return jax.shard_map(
        per_device,
        mesh=mesh,
        in_specs=(P("antb", "anta", "tm"),),
        out_specs=P("tm", None, "anta", "antb", None),
        check_vma=False,
    )
```

```python
import math

import jax
import jax.numpy as jnp
from jax import lax
from jax.experimental import pallas as pl
from jax.experimental.pallas import tpu as pltpu
from jax.sharding import PartitionSpec as P

POLARISATION_NUM = 2
LAG_TOTAL = 256
FINE = 16
PER_STEP = 2
LANES = 128
STRIP = 16


def shift_kernel(row_ref, out_ref):
    window = row_ref.shape[1]
    wide = row_ref[...].astype(jnp.float32)
    wide = jnp.concatenate([wide, jnp.zeros((STRIP, LANES), jnp.float32)], 1)
    for fine in range(FINE):
        out_ref[fine] = wide[:, :window].astype(jnp.bfloat16)
        if fine + 1 < FINE:
            wide = pltpu.roll(wide, 1, 1)


def shifted_rows(rows):
    row_count, window = rows.shape
    out = pl.pallas_call(
        shift_kernel,
        grid=(row_count // STRIP,),
        in_specs=[pl.BlockSpec((STRIP, window), lambda i: (i, 0))],
        out_specs=pl.BlockSpec((FINE, STRIP, window), lambda i: (0, i, 0)),
        out_shape=jax.ShapeDtypeStruct((FINE, row_count, window), jnp.bfloat16),
        compiler_params=pltpu.CompilerParams(vmem_limit_bytes=32 * 1024 * 1024),
        name="shifted_rows",
    )(rows)
    return out.reshape(FINE * row_count, window)


def lag_kernel(shifted_ref, col_ref, *refs, coarse, factor, lag_portion, parts, part_of):
    *prev, out_ref, wide_ref = refs
    stacked, window = shifted_ref.shape
    row_count = stacked // PER_STEP
    col_count = col_ref.shape[1]
    part_chunks = col_count // LANES
    chunks = part_chunks * parts
    lag_start = lax.axis_index("tm") * lag_portion
    first_chunk = part_of() * part_chunks

    @pl.when(pl.program_id(0) == 0)
    def _():
        wide_ref[window:, :] = jnp.zeros((LAG_TOTAL, col_count), jnp.bfloat16)

        def fill_cols(index, carry):
            at = pl.multiple_of(index * LANES, LANES)
            wide_ref[pl.ds(at, LANES), :] = col_ref[pl.ds(at, LANES), :]
            return carry

        lax.fori_loop(0, window // LANES, fill_cols, 0)

    def coarse_lag(step, carry):
        start = pl.multiple_of(lag_start + step * FINE, FINE)
        product = jnp.dot(
            shifted_ref[...], wide_ref[pl.ds(start, window), :], preferred_element_type=jnp.float32
        ) * factor
        for fine in range(PER_STEP):
            if prev:
                out_ref[step, fine] = prev[0][step, fine]
            for chunk in range(part_chunks):
                out_ref[step, fine, pl.ds(first_chunk + chunk, row_count, stride=chunks), :] = product[
                    fine * row_count : (fine + 1) * row_count, chunk * LANES : (chunk + 1) * LANES
                ]
        return carry

    lax.fori_loop(0, coarse, coarse_lag, 0)


def lag_products(shifted, columns, prev, lag_portion, parts, part_of):
    row_count, window = shifted.shape[0] // FINE, shifted.shape[1]
    col_count = columns.shape[1]
    coarse = lag_portion // FINE
    out_rows = row_count * parts * (col_count // LANES)

    def kernel(*refs):
        lag_kernel(
            *refs, coarse=coarse, factor=1.0 / math.sqrt(window), lag_portion=lag_portion,
            parts=parts, part_of=part_of,
        )

    whole = pl.BlockSpec(memory_space=pltpu.VMEM)
    block = pl.BlockSpec((coarse, PER_STEP, out_rows, LANES), lambda m: (0, m, 0, 0))
    return pl.pallas_call(
        kernel,
        grid=(FINE // PER_STEP,),
        in_specs=[pl.BlockSpec((PER_STEP * row_count, window), lambda m: (m, 0)), whole] + [block] * len(prev),
        out_specs=block,
        out_shape=jax.ShapeDtypeStruct((coarse, FINE, out_rows, LANES), jnp.float32),
        scratch_shapes=[
            pltpu.VMEM((window + LAG_TOTAL, col_count), jnp.bfloat16),
        ],
        input_output_aliases={2: 0} if prev else {},
        compiler_params=pltpu.CompilerParams(vmem_limit_bytes=56 * 1024 * 1024),
        name="lag_products",
    )(shifted, columns, *prev)


def swap(array, axis, distance, size):
    return lax.ppermute(array, axis, [(i, (i + distance) % size) for i in range(size)])


def per_device(samples):
    own = samples[0]
    own_antennas, block_len = own.shape
    tm_size = lax.axis_size("tm")
    anta_size = lax.axis_size("anta")
    lag_portion = LAG_TOTAL // tm_size
    antenna_total = own_antennas * anta_size
    half = anta_size // 2
    anta_at = lax.axis_index("anta")

    other = swap(own, "antb", 1, POLARISATION_NUM)
    first = lax.axis_index("antb") == 0
    both = jnp.concatenate([jnp.where(first, own, other), jnp.where(first, other, own)], 0)

    both, turned = lax.optimization_barrier((both, own.T))
    rows = lax.all_gather(both, "tm", axis=1, tiled=True)
    if half == 2:
        pairs = [(i, i ^ 1) for i in range(anta_size)]
        beside = lax.ppermute(turned, "anta", pairs)
        even = anta_at % 2 == 0
        near = jnp.concatenate([jnp.where(even, turned, beside), jnp.where(even, beside, turned)], 1)
    else:
        groups = [list(range(half)), list(range(half, anta_size))]
        near = lax.all_gather(turned, "anta", axis=1, tiled=True, axis_index_groups=groups)
    near_columns = lax.all_gather(near, "tm", axis=0, tiled=True)
    far_columns = swap(near_columns, "anta", half, anta_size)

    def near_part():
        return lax.axis_index("anta") // half

    def far_part():
        return 1 - lax.axis_index("anta") // half

    shifted = shifted_rows(rows)
    out = lag_products(shifted, near_columns, (), lag_portion, 2, near_part)
    out = lag_products(shifted, far_columns, (out,), lag_portion, 2, far_part)
    return out.reshape(lag_portion, POLARISATION_NUM, own_antennas, 1, antenna_total)


def solution(mesh):
    return jax.shard_map(
        per_device,
        mesh=mesh,
        in_specs=(P("antb", "anta", "tm"),),
        out_specs=P("tm", None, "anta", "antb", None),
        check_vma=False,
    )
```
